32 devices in a mesh: tm: 16 (over z, y, core), series: 2 (over x).
Axes of the slice: x: 2, y: 2, z: 4, core: 2. Of those that a mesh axis runs over, the one named last changes fastest.
Arguments:
- panel: bfloat16 [4096, 16384], P('series', 'tm'), may hold values from -6 to 6
- series_factors: bfloat16 [4096, 128], P('series'), may hold values from -1.796875 to 1.796875
- time_factors: bfloat16 [16384, 128], P('tm'), may hold values from -1.796875 to 1.796875
- ar_weights: float32 [16, 128], replicated, may hold values from -1 to 1
- tile_mask: int32 [32, 128], P('series', 'tm'), may hold values 0 or 1
- lags: int32 [16], replicated, may hold values from 1 to 128, as said below
Outputs:
- series_grad: float32 [4096, 128], P(('series', 'tm'))
- time_grad: float32 [16384, 128], P(('tm', 'series'))
- ar_grad: float32 [16, 128], replicated
The draws below stay inside these ranges and needn't reach their ends.
Inputs may be any that keep to these rules, and one draw needn't show every extreme that they name: `lags`: strictly increasing, and the last equals 128.
All inputs are finite; a program needn't handle non-finite values. No bound on the sum of `tile_mask` on one device may be relied on, other than what follows from the above.
Results may differ from the reference program's by a relative error of at most 0.00045.
Values may be sent and summed in bfloat16 or wider, within the bound.
A program may use at most 64 MiB of HBM per device.

```python
import math
import jax
import jax.numpy as jnp
from jax import lax

K = 128
NLAG = 16
LAGMAX = 128
TILE = 128
TD = 1024
NS = 4096
NT = 16384


def draw_lags(key, part):
    picked = jax.random.permutation(key, LAGMAX - 1)[:NLAG - 1] + 1
    full = jnp.concatenate([picked.astype(jnp.int32), jnp.array([LAGMAX], jnp.int32)])
    return jnp.sort(full).astype(jnp.int32)


def plant(values, key, low, high):
    longest = values.shape.index(max(values.shape))
    spots = []
    for shift in (0, 1):
        where = [jax.random.randint(jax.random.fold_in(key, axis), (), 0, length) for axis, length in enumerate(values.shape)]
        where[longest] = (where[longest] + shift) % values.shape[longest]
        spots.append(tuple(where))
    return values.at[spots[0]].set(low).at[spots[1]].set(high)


def shard_levels(stream_key, shape, split, low, top_value):
    gain = 1.0
    for position, blocks in split:
        draws = jax.random.uniform(jax.random.fold_in(jax.random.fold_in(stream_key, 6), position), (blocks,), jnp.float32, low / len(split), top_value / len(split))
        gain = gain * jnp.repeat(jnp.exp(draws), shape[position] // blocks).reshape((-1,) + (1,) * (len(shape) - 1 - position))
    return gain


def noise(key, dims, width, most, shards=(), held_as=jnp.bfloat16):
    drawn = jax.random.normal(key, dims, jnp.float32) * width
    if len(shards) > 0:
        drawn = shard_levels(key, dims, shards, -0.22, 0.18) * drawn
    return jnp.clip(drawn, min=-most, max=most).astype(held_as)


def setup_inputs(seed: int = 0) -> dict:
    seeds = jax.random.split(jax.random.key(seed), 7)
    return {
        "panel": noise(seeds[0], (NS, NT), 1.0, 6.0, ((0, 2), (1, 16))),
        "series_factors": noise(seeds[1], (NS, K), 0.3, 1.796875, ((0, 2),)),
        "time_factors": noise(seeds[2], (NT, K), 0.3, 1.796875, ((0, 16),)),
        "ar_weights": noise(seeds[3], (NLAG, K), 0.25, 1.0, (), jnp.float32),
        "tile_mask": plant((jax.random.randint(seeds[4], (NS // TILE, NT // TILE), 0, 4) < 3).astype(jnp.int32), jax.random.fold_in(seeds[4], 1), 0, 1),
        "lags": draw_lags(jax.random.fold_in(seeds[6], 71), 0),
    }


ar_strength = 1.0

def lag_error(extended, weights, lags, count):
    total = extended[LAGMAX:LAGMAX + count]
    for lag_pos in range(NLAG):
        shifted = lax.dynamic_slice_in_dim(extended, (LAGMAX - lags[lag_pos]).astype(jnp.int32), count, 0)
        total = total - weights[lag_pos] * shifted
    return total

def reference(panel, series_factors, time_factors, ar_weights, tile_mask, lags):
    total_series = panel.shape[0]
    total_time = panel.shape[1]
    rank_width = time_factors.shape[1]
    scale_time = 1.0 / math.sqrt(total_time)
    scale_series = 1.0 / math.sqrt(total_series)
    blocks = total_time // TD

    def one_block(carry, block):
        start = (block * TD).astype(jnp.int32)
        factor_rows = lax.dynamic_slice_in_dim(time_factors, start, TD, 0)
        values = lax.dynamic_slice_in_dim(panel, start, TD, 1)
        mask_cols = lax.dynamic_slice_in_dim(tile_mask, (block * (TD // TILE)).astype(jnp.int32), TD // TILE, 1)
        keep = jnp.repeat(jnp.repeat(mask_cols, TILE, 0), TILE, 1) > 0
        predicted = jnp.dot(series_factors, factor_rows.T, preferred_element_type=jnp.float32)
        residual = jnp.where(keep, predicted - values.astype(jnp.float32), jnp.float32(0.0)).astype(jnp.bfloat16)
        carry = carry + jnp.dot(residual, factor_rows, preferred_element_type=jnp.float32)
        time_part = lax.dot_general(residual, series_factors, (((0,), (0,)), ((), ())), preferred_element_type=jnp.float32)
        return (carry, time_part)
    series_sum, time_parts = lax.scan(one_block, jnp.zeros((total_series, rank_width), jnp.float32), jnp.arange(blocks, dtype=jnp.int32))
    series_grad = series_sum * scale_time
    data_grad = time_parts.reshape(total_time, rank_width) * scale_series
    factors32 = time_factors.astype(jnp.float32)
    extended = jnp.concatenate([jnp.zeros((LAGMAX, rank_width), jnp.float32), factors32], axis=0)
    moments = jnp.arange(total_time, dtype=jnp.int32)
    error = jnp.where((moments >= LAGMAX)[:, None], lag_error(extended, ar_weights, lags, total_time), jnp.float32(0.0))
    error_ext = jnp.concatenate([error, jnp.zeros((LAGMAX, rank_width), jnp.float32)], axis=0)
    adjoint = error
    ar_rows = []
    for lag_pos in range(NLAG):
        ahead = lax.dynamic_slice_in_dim(error_ext, lags[lag_pos].astype(jnp.int32), total_time, 0)
        adjoint = adjoint - ar_weights[lag_pos] * ahead
        behind = lax.dynamic_slice_in_dim(extended, (LAGMAX - lags[lag_pos]).astype(jnp.int32), total_time, 0)
        ar_rows.append(-scale_time * lax.optimization_barrier(jnp.sum(error * behind, axis=0)))
    time_grad = data_grad + ar_strength * adjoint
    ar_grad = jnp.stack(ar_rows)
    return (series_grad, time_grad, ar_grad)
```

```python
import functools
import math

import jax
import jax.numpy as jnp
from jax import lax
from jax.experimental import pallas as pl
from jax.experimental.pallas import tpu as pltpu
from jax.sharding import PartitionSpec as P

NLAG = 16
LAGMAX = 128
TILE = 128
STEP = 64
F32 = jnp.float32
BF16 = jnp.bfloat16


def kernel(
    n, ns, scale_time, scale_series, row_tile,
    lags_ref, mask_ref, panel_ref, s_hbm, f_hbm, w_ref,
    out_s, out_t, out_a,
    pbuf, sbuf, fbuf, g, tt, tsend, trecv, ext, err, hprev, hnext,
    crx, s1, yrx, s2, zrx, ar0, ar1, arc, ary, arz,
    psem, insem, hsem, tsem, csem, ysem, zsem, acsem, aysem, azsem,
):
    rows, cols = pbuf.shape
    nz = n // 4
    block = rows // n
    chunk = rows // nz
    width = cols // ns
    part = rows // 4
    me = lax.axis_index("tm")
    my_s = lax.axis_index("series")
    c = lax.rem(me, 2)
    y = lax.rem(lax.div(me, 2), 2)
    z = lax.div(me, 4)
    core_peer = {"tm": me + 1 - 2 * c}
    y_peer = {"tm": me + 2 - 4 * y}
    low = lax.rem(me, 4)
    has_prev = me > 0
    has_next = me < n - 1
    other = me - 1 + 2 * c
    has_other = jnp.logical_and(other >= 0, other < n)

    def z_peer(i):
        return {"tm": lax.rem(z + 1 + i, nz) * 4 + low}

    def s_peer(o):
        return {"series": lax.rem(my_s + o, ns)}

    def remote(src, dst, sem, target):
        return pltpu.make_async_remote_copy(
            src_ref=src, dst_ref=dst, send_sem=sem.at[0], recv_sem=sem.at[1],
            device_id=target, device_id_type=pl.DeviceIdType.MESH)

    barrier = pltpu.get_barrier_semaphore()

    def greet(target):
        pl.semaphore_signal(barrier, inc=1, device_id=target,
                            device_id_type=pl.DeviceIdType.MESH)

    greet(core_peer)
    greet(y_peer)
    for i in range(nz - 1):
        greet(z_peer(i))
    for o in range(1, ns):
        greet(s_peer(o))

    @pl.when(has_other)
    def _():
        greet({"tm": other})

    load_s = pltpu.make_async_copy(s_hbm, sbuf, insem.at[0])
    load_f = pltpu.make_async_copy(f_hbm, fbuf, insem.at[1])
    load_s.start()
    load_f.start()

    def col0(o):
        return pl.multiple_of(lax.rem(my_s + o, ns) * width, TILE)

    def panel_load(o, k):
        window = (pl.ds(k * part, part), pl.ds(col0(o), width))
        return pltpu.make_async_copy(
            panel_ref.at[window], pbuf.at[window], psem.at[o, k])

    order = list(range(1, ns)) + [0]
    for o in order:
        for k in range(4):
            panel_load(o, k).start()
    load_s.wait()
    load_f.wait()

    def tile(o, r0, first):
        r0 = pl.multiple_of(r0, row_tile)
        c0 = col0(o)
        s = sbuf[pl.ds(r0, row_tile), :]
        f = fbuf[pl.ds(c0, width), :]
        pred = lax.dot_general(s, f, (((1,), (1,)), ((), ())), preferred_element_type=F32)
        diff = pred - pbuf[pl.ds(r0, row_tile), pl.ds(c0, width)].astype(F32)
        mr, mc = lax.div(r0, TILE), lax.div(c0, TILE)
        pieces = []
        for a in range(row_tile // TILE):
            keep = jnp.concatenate(
                [jnp.full((TILE, TILE), mask_ref[mr + a, mc + b], jnp.int32)
                 for b in range(width // TILE)], axis=1) > 0
            pieces.append(jnp.where(keep, diff[a * TILE:(a + 1) * TILE], 0.0))
        res = jnp.concatenate(pieces, axis=0).astype(BF16)
        add = jnp.dot(res, f, preferred_element_type=F32)
        if first:
            g[pl.ds(r0, row_tile), :] = add
        else:
            g[pl.ds(r0, row_tile), :] += add
        tt[o] += lax.dot_general(s, res, (((0,), (0,)), ((), ())), preferred_element_type=F32)

    def tiles(o, start, count, first):
        def body(k, carry):
            tile(o, start + k * row_tile, first)
            return carry
        lax.fori_loop(0, count, body, 0)

    tt[...] = jnp.zeros_like(tt)
    to_next = remote(fbuf.at[pl.ds(cols - LAGMAX, LAGMAX)], hprev, hsem.at[0],
                     {"tm": lax.min(me + 1, n - 1)})
    to_prev = remote(fbuf.at[pl.ds(0, LAGMAX)], hnext, hsem.at[1],
                     {"tm": lax.max(me - 1, 0)})
    tcopies = []
    for o in range(1, ns):
        for k in range(4):
            panel_load(o, k).wait()
            tiles(o, k * part, part // row_tile, o == 1)
            if o == 1 and k == 0:
                base = 1 + 1 + (nz - 1) + (ns - 1)
                pl.semaphore_wait(barrier, base + has_other.astype(jnp.int32))

                @pl.when(has_next)
                def _():
                    to_next.start()

                @pl.when(has_prev)
                def _():
                    to_prev.start()
        tsend[o - 1] = tt[o].T
        copy = remote(tsend.at[o - 1], trecv.at[o - 1], tsem.at[o - 1], s_peer(o))
        copy.start()
        tcopies.append(copy)

    ext[pl.ds(LAGMAX, cols), :] = fbuf[...].astype(F32)

    @pl.when(has_next)
    def _():
        to_next.wait_send()
        to_prev.wait_recv()
        ext[pl.ds(LAGMAX + cols, LAGMAX), :] = hnext[...].astype(F32)

    @pl.when(jnp.logical_not(has_next))
    def _():
        ext[pl.ds(LAGMAX + cols, LAGMAX), :] = jnp.zeros((LAGMAX, w_ref.shape[1]), F32)

    @pl.when(has_prev)
    def _():
        to_prev.wait_send()
        to_next.wait_recv()
        ext[pl.ds(0, LAGMAX), :] = hprev[...].astype(F32)

    @pl.when(jnp.logical_not(has_prev))
    def _():
        ext[pl.ds(0, LAGMAX), :] = jnp.zeros((LAGMAX, w_ref.shape[1]), F32)

    lags = [lags_ref[j] for j in range(NLAG)]
    rank = w_ref.shape[1]

    def error_tile(t0):
        total = ext[pl.ds(t0 + LAGMAX, STEP), :]
        for j in range(NLAG):
            total = total - w_ref[pl.ds(j, 1), :] * ext[pl.ds(t0 + LAGMAX - lags[j], STEP), :]
        return total

    def prior_body(k, sums):
        t0 = pl.multiple_of(k * STEP, STEP)
        live = jnp.logical_or(has_prev, t0 >= LAGMAX).astype(F32)
        total = error_tile(t0)
        total = jnp.where(jnp.full(total.shape, live) > 0, total, 0.0)
        err[pl.ds(t0, STEP), :] = total
        new = []
        for j in range(NLAG):
            prod = total * ext[pl.ds(t0 + LAGMAX - lags[j], STEP), :]
            new.append(sums[j] + prod.reshape(STEP // 8, 8, rank).sum(axis=0))
        return tuple(new)

    sums = lax.fori_loop(0, cols // STEP, prior_body,
                         tuple(jnp.zeros((8, rank), F32) for _ in range(NLAG)))

    def tail_body(k, carry):
        t0 = pl.multiple_of(cols + k * STEP, STEP)
        total = error_tile(t0)
        live = jnp.full(total.shape, has_next.astype(F32))
        err[pl.ds(t0, STEP), :] = jnp.where(live > 0, total, 0.0)
        return carry

    ar0[...] = jnp.concatenate([s.sum(axis=0, keepdims=True) for s in sums], axis=0)
    ar_core = remote(ar0, arc, acsem, core_peer)
    ar_core.start()
    lax.fori_loop(0, LAGMAX // STEP, tail_body, 0)

    def core_copy(i):
        q = lax.rem(z + 1 + i, nz)
        return remote(g4.at[q, :, 1 - c], crx.at[i], csem.at[i], core_peer)

    def y_copy(i):
        return remote(s1.at[i, 1 - y], yrx.at[i], ysem.at[i], y_peer)

    def z_copy(i):
        return remote(s2.at[i], zrx.at[i], zsem.at[i], z_peer(i))

    g4 = g.reshape(nz, 2, 2, block, rank)

    def after_core(i):
        q = lax.rem(z + 1 + i, nz)
        core_copy(i).wait()
        for b in range(2):
            s1[i, b] = g4[q, b, c] + crx[i, b]
        y_copy(i).start()

    def after_y(i):
        y_copy(i).wait()
        s2[i] = s1[i, y] + yrx[i]
        if i < nz - 1:
            z_copy(i).start()

    ar_y = remote(ar1, ary, aysem, y_peer)
    az = [remote(arz.at[z], arz.at[z], azsem.at[i], z_peer(i)) for i in range(nz - 1)]
    for k in range(4):
        panel_load(0, k).wait()
    for i in range(nz):
        q = lax.rem(z + 1 + i, nz)
        tiles(0, q * chunk, chunk // row_tile, ns == 1)
        core_copy(i).start()
        if i == 0:
            ar_core.wait()
            ar1[...] = ar0[...] + arc[...]
            ar_y.start()
        if i >= 1:
            after_core(i - 1)
        if i == min(1, nz - 1):
            ar_y.wait()
            arz[z] = ar1[...] + ary[...]
            for copy in az:
                copy.start()
        if i >= 2:
            after_y(i - 2)
    if nz >= 2:
        after_y(nz - 2)
    after_core(nz - 1)

    own = tt[0].T
    tsend[ns - 1] = own
    for copy in tcopies:
        copy.wait()
    own0 = my_s * width

    def out_body(k, carry):
        t0 = pl.multiple_of(k * STEP, STEP)
        base = pl.multiple_of(own0 + t0, STEP)
        adj = err[pl.ds(base, STEP), :]
        for j in range(NLAG):
            adj = adj - w_ref[pl.ds(j, 1), :] * err[pl.ds(base + lags[j], STEP), :]
        data = tsend[ns - 1, pl.ds(t0, STEP), :]
        for o in range(1, ns):
            data = data + trecv[o - 1, pl.ds(t0, STEP), :]
        out_t[pl.ds(t0, STEP), :] = data * scale_series + adj
        return carry

    lax.fori_loop(0, width // STEP, out_body, 0)

    for copy in az:
        copy.wait()
    total = arz[0]
    for k in range(1, nz):
        total = total + arz[k]
    out_a[...] = total * (-scale_time)

    after_y(nz - 1)
    total = s2[nz - 1]
    for i in range(nz - 1):
        z_copy(i).wait()
        total = total + zrx[i]
    out_s[...] = total * scale_time


def per_device(panel, series_factors, time_factors, ar_weights, tile_mask, lags):
    rows, cols = panel.shape
    rank = series_factors.shape[1]
    n = lax.axis_size("tm")
    ns = lax.axis_size("series")
    nz = n // 4
    block = rows // n
    width = cols // ns
    row_tile = min(2 * TILE, rows // nz)
    any_space = pl.BlockSpec(memory_space=pl.ANY)
    smem = pl.BlockSpec(memory_space=pltpu.SMEM)
    vmem = pl.BlockSpec(memory_space=pltpu.VMEM)
    dma = pltpu.SemaphoreType.DMA
    body = functools.partial(
        kernel, n, ns, 1.0 / math.sqrt(cols * n), 1.0 / math.sqrt(rows * ns), row_tile)
    return pl.pallas_call(
        body,
        out_shape=(
            jax.ShapeDtypeStruct((block, rank), F32),
            jax.ShapeDtypeStruct((width, rank), F32),
            jax.ShapeDtypeStruct((NLAG, rank), F32),
        ),
        in_specs=[smem, smem, any_space, any_space, any_space, vmem],
        out_specs=(vmem, vmem, vmem),
        scratch_shapes=[
            pltpu.VMEM((rows, cols), BF16),
            pltpu.VMEM((rows, rank), BF16),
            pltpu.VMEM((cols, rank), BF16),
            pltpu.VMEM((rows, rank), F32),
            pltpu.VMEM((ns, rank, width), F32),
            pltpu.VMEM((ns, width, rank), F32),
            pltpu.VMEM((max(ns - 1, 1), width, rank), F32),
            pltpu.VMEM((cols + 2 * LAGMAX, rank), F32),
            pltpu.VMEM((cols + LAGMAX, rank), F32),
            pltpu.VMEM((LAGMAX, rank), BF16),
            pltpu.VMEM((LAGMAX, rank), BF16),
            pltpu.VMEM((nz, 2, block, rank), F32),
            pltpu.VMEM((nz, 2, block, rank), F32),
            pltpu.VMEM((nz, block, rank), F32),
            pltpu.VMEM((nz, block, rank), F32),
            pltpu.VMEM((max(nz - 1, 1), block, rank), F32),
            pltpu.VMEM((NLAG, rank), F32),
            pltpu.VMEM((NLAG, rank), F32),
            pltpu.VMEM((NLAG, rank), F32),
            pltpu.VMEM((NLAG, rank), F32),
            pltpu.VMEM((nz, NLAG, rank), F32),
            dma((ns, 4)),
            dma((2,)),
            dma((2, 2)),
            dma((max(ns - 1, 1), 2)),
            dma((nz, 2)),
            dma((nz, 2)),
            dma((max(nz - 1, 1), 2)),
            dma((2,)),
            dma((2,)),
            dma((max(nz - 1, 1), 2)),
        ],
        compiler_params=pltpu.CompilerParams(collective_id=0, has_side_effects=True),
        name="factor_grad",
    )(lags, tile_mask, panel, series_factors, time_factors, ar_weights)


def solution(mesh):
    in_specs = (P("series", "tm"), P("series", None), P("tm", None), P(), P("series", "tm"), P())
    out_specs = (P(("series", "tm"), None), P(("tm", "series"), None), P())
    return jax.shard_map(
        per_device, mesh=mesh, in_specs=in_specs, out_specs=out_specs, check_vma=False
    )
```

```python
import functools
import math

import jax
import jax.numpy as jnp
from jax import lax
from jax.experimental import pallas as pl
from jax.experimental.pallas import tpu as pltpu
from jax.sharding import PartitionSpec as P

NLAG = 16
LAGMAX = 128
TILE = 128
STEP = 64
F32 = jnp.float32
BF16 = jnp.bfloat16


def kernel(
    n, ns, scale_time, scale_series, row_tile,
    lags_hbm, mask_hbm, panel_ref, s_hbm, f_hbm, w_hbm,
    out_s, out_t, out_a,
    lags_ref, mask_ref, w_ref, pbuf, sbuf, fbuf, g, tt, tsend, own, trecv, ext, err, hprev, hnext,
    crx, s1, yrx, s2, zrx, ar0, ar1, arc, ary, arz,
    psem, insem, hsem, tsem, csem, ysem, zsem, acsem, aysem, azsem,
):
    rows, cols = pbuf.shape
    nz = n // 4
    block = rows // n
    chunk = rows // nz
    width = cols // ns
    me = lax.axis_index("tm")
    my_s = lax.axis_index("series")
    c = lax.rem(me, 2)
    y = lax.rem(lax.div(me, 2), 2)
    z = lax.div(me, 4)
    core_peer = {"tm": me + 1 - 2 * c}
    y_peer = {"tm": me + 2 - 4 * y}
    low = lax.rem(me, 4)
    has_prev = me > 0
    has_next = me < n - 1
    other = me - 1 + 2 * c
    has_other = jnp.logical_and(other >= 0, other < n)

    def z_peer(i):
        return {"tm": lax.rem(z + 1 + i, nz) * 4 + low}

    def s_peer(o):
        return {"series": lax.rem(my_s + o, ns)}

    def remote(src, dst, sem, target):
        return pltpu.make_async_remote_copy(
            src_ref=src, dst_ref=dst, send_sem=sem.at[0], recv_sem=sem.at[1],
            device_id=target, device_id_type=pl.DeviceIdType.MESH)

    barrier = pltpu.get_barrier_semaphore()

    def greet(target):
        pl.semaphore_signal(barrier, inc=1, device_id=target,
                            device_id_type=pl.DeviceIdType.MESH)

    greet(core_peer)
    greet(y_peer)
    for i in range(nz - 1):
        greet(z_peer(i))
    for o in range(1, ns):
        greet(s_peer(o))

    @pl.when(has_other)
    def _():
        greet({"tm": other})

    loads = [pltpu.make_async_copy(a, b, insem.at[k]) for k, (a, b) in enumerate(
        [(s_hbm, sbuf), (f_hbm, fbuf), (mask_hbm, mask_ref), (w_hbm, w_ref), (lags_hbm, lags_ref)])]

    def place(i):
        return lax.rem(z + 1 + i, nz)

    def panel_load(i):
        window = (pl.ds(place(i) * chunk, chunk), slice(None))
        return pltpu.make_async_copy(panel_ref.at[window], pbuf.at[window], psem.at[i])

    for k in range(3):
        loads[k].start()
    panel_load(0).start()
    loads[3].start()
    loads[4].start()
    for i in range(1, nz):
        panel_load(i).start()
    tt[...] = jnp.zeros_like(tt)
    for k in range(3):
        loads[k].wait()

    def tile(r0):
        r0 = pl.multiple_of(r0, row_tile)
        s = sbuf[pl.ds(r0, row_tile), :]
        f = fbuf[...]
        mr = lax.div(r0, TILE)
        pred = lax.dot_general(s, f, (((1,), (1,)), ((), ())), preferred_element_type=F32)
        diff = pred - pbuf[pl.ds(r0, row_tile), :].astype(F32)
        pieces = []
        for a in range(row_tile // TILE):
            keep = jnp.concatenate(
                [jnp.full((TILE, TILE), mask_ref[b, mr + a], jnp.int32)
                 for b in range(cols // TILE)], axis=1) > 0
            pieces.append(jnp.where(keep, diff[a * TILE:(a + 1) * TILE], 0.0))
        res = jnp.concatenate(pieces, axis=0).astype(BF16)
        g[pl.ds(r0, row_tile), :] = jnp.dot(res, f, preferred_element_type=F32)
        add = lax.dot_general(s, res, (((0,), (0,)), ((), ())), preferred_element_type=F32)
        for k in range(ns):
            tt[k] += add[:, k * width:(k + 1) * width]

    def tiles(i):
        start = place(i) * chunk
        panel_load(i).wait()

        def body(k, carry):
            tile(start + k * row_tile)
            return carry
        lax.fori_loop(0, chunk // row_tile, body, 0)

    to_next = remote(fbuf.at[pl.ds(cols - LAGMAX, LAGMAX)], hprev, hsem.at[0],
                     {"tm": lax.min(me + 1, n - 1)})
    to_prev = remote(fbuf.at[pl.ds(0, LAGMAX)], hnext, hsem.at[1],
                     {"tm": lax.max(me - 1, 0)})
    rank = w_ref.shape[1]
    g4 = g.reshape(nz, 2, 2, block, rank)

    def core_copy(i):
        return remote(g4.at[place(i), :, 1 - c], crx.at[i], csem.at[i], core_peer)

    def y_copy(i):
        return remote(s1.at[i, 1 - y], yrx.at[i], ysem.at[i], y_peer)

    def z_copy(i):
        return remote(s2.at[i], zrx.at[i], zsem.at[i], z_peer(i))

    def after_core(i):
        core_copy(i).wait()
        for b in range(2):
            s1[i, b] = g4[place(i), b, c] + crx[i, b]
        y_copy(i).start()

    def after_y(i):
        y_copy(i).wait()
        s2[i] = s1[i, y] + yrx[i]
        if i < nz - 1:
            z_copy(i).start()

    tcopies = [remote(tsend.at[o - 1], trecv.at[o - 1], tsem.at[o - 1], s_peer(o))
               for o in range(1, ns)]
    ar_core = remote(ar0, arc, acsem, core_peer)
    ar_y = remote(ar1, ary, aysem, y_peer)
    az = [remote(arz.at[z], arz.at[z], azsem.at[i], z_peer(i)) for i in range(nz - 1)]

    def error_tile(t0, lags):
        total = ext[pl.ds(t0 + LAGMAX, STEP), :]
        for j in range(NLAG):
            total = total - w_ref[pl.ds(j, 1), :] * ext[pl.ds(t0 + LAGMAX - lags[j], STEP), :]
        return total

    def all_lags():
        return [lags_ref[j] for j in range(NLAG)]

    def prior_start():
        loads[3].wait()
        loads[4].wait()
        ext[pl.ds(LAGMAX, cols), :] = fbuf[...].astype(F32)
        blank = jnp.zeros((LAGMAX, rank), F32)

        @pl.when(has_next)
        def _():
            to_next.wait_send()
            to_prev.wait_recv()
            ext[pl.ds(LAGMAX + cols, LAGMAX), :] = hnext[...].astype(F32)

        @pl.when(jnp.logical_not(has_next))
        def _():
            ext[pl.ds(LAGMAX + cols, LAGMAX), :] = blank

        @pl.when(has_prev)
        def _():
            to_prev.wait_send()
            to_next.wait_recv()
            ext[pl.ds(0, LAGMAX), :] = hprev[...].astype(F32)

        @pl.when(jnp.logical_not(has_prev))
        def _():
            ext[pl.ds(0, LAGMAX), :] = blank

        lags = all_lags()

        def body(k, sums):
            t0 = pl.multiple_of(k * STEP, STEP)
            live = jnp.logical_or(has_prev, t0 >= LAGMAX).astype(F32)
            total = error_tile(t0, lags)
            total = jnp.where(jnp.full(total.shape, live) > 0, total, 0.0)
            err[pl.ds(t0, STEP), :] = total
            new = []
            for j in range(NLAG):
                prod = total * ext[pl.ds(t0 + LAGMAX - lags[j], STEP), :]
                new.append(sums[j] + prod.reshape(STEP // 8, 8, rank).sum(axis=0))
            return tuple(new)

        sums = lax.fori_loop(0, cols // STEP, body,
                             tuple(jnp.zeros((8, rank), F32) for _ in range(NLAG)))
        ar0[...] = jnp.concatenate([s.sum(axis=0, keepdims=True) for s in sums], axis=0)
        ar_core.start()

    def adjoint():
        lags = all_lags()

        def tail(k, carry):
            t0 = pl.multiple_of(cols + k * STEP, STEP)
            total = error_tile(t0, lags)
            live = jnp.full(total.shape, has_next.astype(F32))
            err[pl.ds(t0, STEP), :] = jnp.where(live > 0, total, 0.0)
            return carry

        def body(k, carry):
            t0 = pl.multiple_of(k * STEP, STEP)
            base = pl.multiple_of(my_s * width + t0, STEP)
            adj = err[pl.ds(base, STEP), :]
            for j in range(NLAG):
                adj = adj - w_ref[pl.ds(j, 1), :] * err[pl.ds(base + lags[j], STEP), :]
            own[pl.ds(t0, STEP), :] += adj
            return carry

        lax.fori_loop(0, LAGMAX // STEP, tail, 0)
        lax.fori_loop(0, width // STEP, body, 0)

    for i in range(nz):
        if i == nz - 1:
            prior_start()
            if i >= 1:
                after_core(i - 1)
        tiles(i)
        if i == 0:
            base = 1 + 1 + (nz - 1) + (ns - 1)
            pl.semaphore_wait(barrier, base + has_other.astype(jnp.int32))

            @pl.when(has_next)
            def _():
                to_next.start()

            @pl.when(has_prev)
            def _():
                to_prev.start()
        core_copy(i).start()
        if i == nz - 1:
            for o in range(1, ns):
                tsend[o - 1] = tt[lax.rem(my_s + o, ns)].T
                tcopies[o - 1].start()
        elif i >= 1:
            after_core(i - 1)
        if i >= 3:
            after_y(i - 3)
    ar_core.wait()
    ar1[...] = ar0[...] + arc[...]
    ar_y.start()
    after_core(nz - 1)
    if nz >= 3:
        after_y(nz - 3)
    own[...] = tt[my_s].T * scale_series
    adjoint()
    if nz >= 2:
        after_y(nz - 2)
    ar_y.wait()
    arz[z] = ar1[...] + ary[...]
    for copy in az:
        copy.start()
    after_y(nz - 1)
    for copy in tcopies:
        copy.wait()
    data = own[...]
    for o in range(1, ns):
        data = data + trecv[o - 1] * scale_series
    out_t[...] = data
    for copy in az:
        copy.wait()
    total = arz[0]
    for k in range(1, nz):
        total = total + arz[k]
    out_a[...] = total * (-scale_time)
    total = s2[nz - 1]
    for i in range(nz - 1):
        z_copy(i).wait()
        total = total + zrx[i]
    out_s[...] = total * scale_time


def put_out(*refs):
    sem = refs[-1]
    copies = [pltpu.make_async_copy(refs[k], refs[3 + k], sem.at[k]) for k in range(3)]
    for copy in copies:
        copy.start()
    for copy in copies:
        copy.wait()


def per_device(panel, series_factors, time_factors, ar_weights, tile_mask, lags):
    rows, cols = panel.shape
    rank = series_factors.shape[1]
    n = lax.axis_size("tm")
    ns = lax.axis_size("series")
    nz = n // 4
    block = rows // n
    width = cols // ns
    row_tile = min(2 * TILE, rows // nz)
    any_space = pl.BlockSpec(memory_space=pl.ANY)
    vmem = pl.BlockSpec(memory_space=pltpu.VMEM)
    dma = pltpu.SemaphoreType.DMA
    body = functools.partial(
        kernel, n, ns, 1.0 / math.sqrt(cols * n), 1.0 / math.sqrt(rows * ns), row_tile)
    shapes = ((block, rank), (width, rank), (NLAG, rank))
    results = pl.pallas_call(
        body,
        out_shape=tuple(pltpu.VMEM(shape, F32) for shape in shapes),
        in_specs=[any_space] * 6,
        out_specs=(vmem, vmem, vmem),
        scratch_shapes=[
            pltpu.SMEM((NLAG,), jnp.int32),
            pltpu.SMEM(tile_mask.shape[::-1], jnp.int32),
            pltpu.VMEM((NLAG, rank), F32),
            pltpu.VMEM((rows, cols), BF16),
            pltpu.VMEM((rows, rank), BF16),
            pltpu.VMEM((cols, rank), BF16),
            pltpu.VMEM((rows, rank), F32),
            pltpu.VMEM((ns, rank, width), F32),
            pltpu.VMEM((max(ns - 1, 1), width, rank), F32),
            pltpu.VMEM((width, rank), F32),
            pltpu.VMEM((max(ns - 1, 1), width, rank), F32),
            pltpu.VMEM((cols + 2 * LAGMAX, rank), F32),
            pltpu.VMEM((cols + LAGMAX, rank), F32),
            pltpu.VMEM((LAGMAX, rank), BF16),
            pltpu.VMEM((LAGMAX, rank), BF16),
            pltpu.VMEM((nz, 2, block, rank), F32),
            pltpu.VMEM((nz, 2, block, rank), F32),
            pltpu.VMEM((nz, block, rank), F32),
            pltpu.VMEM((nz, block, rank), F32),
            pltpu.VMEM((max(nz - 1, 1), block, rank), F32),
            pltpu.VMEM((NLAG, rank), F32),
            pltpu.VMEM((NLAG, rank), F32),
            pltpu.VMEM((NLAG, rank), F32),
            pltpu.VMEM((NLAG, rank), F32),
            pltpu.VMEM((nz, NLAG, rank), F32),
            dma((nz,)),
            dma((5,)),
            dma((2, 2)),
            dma((max(ns - 1, 1), 2)),
            dma((nz, 2)),
            dma((nz, 2)),
            dma((max(nz - 1, 1), 2)),
            dma((2,)),
            dma((2,)),
            dma((max(nz - 1, 1), 2)),
        ],
        compiler_params=pltpu.CompilerParams(collective_id=0, has_side_effects=True),
        name="factor_grad",
    )(lags, tile_mask.T, panel, series_factors, time_factors, ar_weights)
    return pl.pallas_call(
        put_out,
        out_shape=tuple(jax.ShapeDtypeStruct(shape, F32) for shape in shapes),
        in_specs=[vmem] * 3,
        out_specs=(any_space,) * 3,
        scratch_shapes=[dma((3,))],
        name="put_out",
    )(*[pltpu.with_memory_space_constraint(r, pltpu.VMEM) for r in results])


def solution(mesh):
    in_specs = (P("series", "tm"), P("series", None), P("tm", None), P(), P("series", "tm"), P())
    out_specs = (P(("series", "tm"), None), P(("tm", "series"), None), P())
    return jax.shard_map(
        per_device, mesh=mesh, in_specs=in_specs, out_specs=out_specs, check_vma=False
    )
```

```python
import functools
import math

import jax
import jax.numpy as jnp
from jax import lax
from jax.experimental import pallas as pl
from jax.experimental.pallas import tpu as pltpu
from jax.sharding import PartitionSpec as P

NLAG = 16
LAGMAX = 128
TILE = 128
STEP = 64
F32 = jnp.float32
BF16 = jnp.bfloat16


LEVELS = 32767.0


def code(value):
    top = jnp.maximum(jnp.max(jnp.abs(value), axis=0, keepdims=True), 1e-30)
    levels = jnp.round(value * (LEVELS / top)).astype(jnp.int32).astype(jnp.int16)
    return levels, jnp.broadcast_to(top * (1.0 / LEVELS), (8, value.shape[1]))


def decode(levels, step):
    return levels.astype(jnp.int32).astype(F32) * step[0:1]


def kernel(
    n, ns, scale_time, scale_series, row_tile,
    lags_hbm, mask_hbm, panel_ref, s_hbm, f_hbm, w_hbm,
    out_s, out_t, out_a,
    lags_ref, mask_ref, w_ref, pbuf, sbuf, fbuf, g, tt, tsend, tstep, own, trecv, trstep, ext, err, hprev, hnext,
    crx, s1, ysend, ystep, yrx, yrstep, s2, zsend, zstep, zrx, zrstep, ar0, ar1, arc, ary, arz,
    psem, insem, hsem, tsem, csem, ysem, zsem, tsem2, ysem2, zsem2, acsem, aysem, azsem,
):
    rows, cols = pbuf.shape
    nz = n // 4
    block = rows // n
    chunk = rows // nz
    width = cols // ns
    me = lax.axis_index("tm")
    my_s = lax.axis_index("series")
    c = lax.rem(me, 2)
    y = lax.rem(lax.div(me, 2), 2)
    z = lax.div(me, 4)
    core_peer = {"tm": me + 1 - 2 * c}
    y_peer = {"tm": me + 2 - 4 * y}
    low = lax.rem(me, 4)
    has_prev = me > 0
    has_next = me < n - 1
    other = me - 1 + 2 * c
    has_other = jnp.logical_and(other >= 0, other < n)

    def z_peer(i):
        return {"tm": lax.rem(z + 1 + i, nz) * 4 + low}

    def s_peer(o):
        return {"series": lax.rem(my_s + o, ns)}

    def remote(src, dst, sem, target):
        return pltpu.make_async_remote_copy(
            src_ref=src, dst_ref=dst, send_sem=sem.at[0], recv_sem=sem.at[1],
            device_id=target, device_id_type=pl.DeviceIdType.MESH)

    barrier = pltpu.get_barrier_semaphore()

    def greet(target):
        pl.semaphore_signal(barrier, inc=1, device_id=target,
                            device_id_type=pl.DeviceIdType.MESH)

    greet(core_peer)
    greet(y_peer)
    for i in range(nz - 1):
        greet(z_peer(i))
    for o in range(1, ns):
        greet(s_peer(o))

    @pl.when(has_other)
    def _():
        greet({"tm": other})

    loads = [pltpu.make_async_copy(a, b, insem.at[k]) for k, (a, b) in enumerate(
        [(s_hbm, sbuf), (f_hbm, fbuf), (mask_hbm, mask_ref), (w_hbm, w_ref), (lags_hbm, lags_ref)])]

    def place(i):
        return lax.rem(z + 1 + i, nz)

    def panel_load(i):
        window = (pl.ds(place(i) * chunk, chunk), slice(None))
        return pltpu.make_async_copy(panel_ref.at[window], pbuf.at[window], psem.at[i])

    for k in range(3):
        loads[k].start()
    panel_load(0).start()
    loads[3].start()
    loads[4].start()
    for i in range(1, nz):
        panel_load(i).start()
    tt[...] = jnp.zeros_like(tt)
    for k in range(3):
        loads[k].wait()

    def tile(r0):
        r0 = pl.multiple_of(r0, row_tile)
        s = sbuf[pl.ds(r0, row_tile), :]
        f = fbuf[...]
        mr = lax.div(r0, TILE)
        pred = lax.dot_general(s, f, (((1,), (1,)), ((), ())), preferred_element_type=F32)
        diff = pred - pbuf[pl.ds(r0, row_tile), :].astype(F32)
        pieces = []
        for a in range(row_tile // TILE):
            keep = jnp.concatenate(
                [jnp.full((TILE, TILE), mask_ref[b, mr + a], jnp.int32)
                 for b in range(cols // TILE)], axis=1) > 0
            pieces.append(jnp.where(keep, diff[a * TILE:(a + 1) * TILE], 0.0))
        res = jnp.concatenate(pieces, axis=0).astype(BF16)
        g[pl.ds(r0, row_tile), :] = jnp.dot(res, f, preferred_element_type=F32)
        add = lax.dot_general(s, res, (((0,), (0,)), ((), ())), preferred_element_type=F32)
        for k in range(ns):
            tt[k] += add[:, k * width:(k + 1) * width]

    def tiles(i):
        start = place(i) * chunk
        panel_load(i).wait()

        def body(k, carry):
            tile(start + k * row_tile)
            return carry
        lax.fori_loop(0, chunk // row_tile, body, 0)

    to_next = remote(fbuf.at[pl.ds(cols - LAGMAX, LAGMAX)], hprev, hsem.at[0],
                     {"tm": lax.min(me + 1, n - 1)})
    to_prev = remote(fbuf.at[pl.ds(0, LAGMAX)], hnext, hsem.at[1],
                     {"tm": lax.max(me - 1, 0)})
    rank = w_ref.shape[1]
    g4 = g.reshape(nz, 2, 2, block, rank)

    def core_copy(i):
        return remote(g4.at[place(i), :, 1 - c], crx.at[i], csem.at[i], core_peer)

    def both(levels, step, lrecv, srecv, lsem, ssem, target):
        return (remote(levels, lrecv, lsem, target), remote(step, srecv, ssem, target))

    def y_copy(i):
        return both(ysend.at[i], ystep.at[i], yrx.at[i], yrstep.at[i],
                    ysem.at[i], ysem2.at[i], y_peer)

    def z_copy(i):
        return both(zsend.at[i], zstep.at[i], zrx.at[i], zrstep.at[i],
                    zsem.at[i], zsem2.at[i], z_peer(i))

    def after_core(i):
        core_copy(i).wait()
        ysend[i], ystep[i] = code(g4[place(i), 1 - y, c] + crx[i, 1 - y])
        for copy in y_copy(i):
            copy.start()
        s1[i] = g4[place(i), y, c] + crx[i, y]

    def after_y(i):
        for copy in y_copy(i):
            copy.wait()
        total = s1[i] + decode(yrx[i], yrstep[i])
        if i < nz - 1:
            zsend[i], zstep[i] = code(total)
            for copy in z_copy(i):
                copy.start()
        else:
            s2[...] = total

    tcopies = [both(tsend.at[o - 1], tstep.at[o - 1], trecv.at[o - 1], trstep.at[o - 1],
                    tsem.at[o - 1], tsem2.at[o - 1], s_peer(o)) for o in range(1, ns)]
    ar_core = remote(ar0, arc, acsem, core_peer)
    ar_y = remote(ar1, ary, aysem, y_peer)
    az = [remote(arz.at[z], arz.at[z], azsem.at[i], z_peer(i)) for i in range(nz - 1)]

    def error_tile(t0, lags):
        total = ext[pl.ds(t0 + LAGMAX, STEP), :]
        for j in range(NLAG):
            total = total - w_ref[pl.ds(j, 1), :] * ext[pl.ds(t0 + LAGMAX - lags[j], STEP), :]
        return total

    def all_lags():
        return [lags_ref[j] for j in range(NLAG)]

    def prior_start():
        loads[3].wait()
        loads[4].wait()
        ext[pl.ds(LAGMAX, cols), :] = fbuf[...].astype(F32)
        blank = jnp.zeros((LAGMAX, rank), F32)

        @pl.when(has_next)
        def _():
            to_next.wait_send()
            to_prev.wait_recv()
            ext[pl.ds(LAGMAX + cols, LAGMAX), :] = hnext[...].astype(F32)

        @pl.when(jnp.logical_not(has_next))
        def _():
            ext[pl.ds(LAGMAX + cols, LAGMAX), :] = blank

        @pl.when(has_prev)
        def _():
            to_prev.wait_send()
            to_next.wait_recv()
            ext[pl.ds(0, LAGMAX), :] = hprev[...].astype(F32)

        @pl.when(jnp.logical_not(has_prev))
        def _():
            ext[pl.ds(0, LAGMAX), :] = blank

        lags = all_lags()

        def body(k, sums):
            t0 = pl.multiple_of(k * STEP, STEP)
            live = jnp.logical_or(has_prev, t0 >= LAGMAX).astype(F32)
            total = error_tile(t0, lags)
            total = jnp.where(jnp.full(total.shape, live) > 0, total, 0.0)
            err[pl.ds(t0, STEP), :] = total
            new = []
            for j in range(NLAG):
                prod = total * ext[pl.ds(t0 + LAGMAX - lags[j], STEP), :]
                new.append(sums[j] + prod.reshape(STEP // 8, 8, rank).sum(axis=0))
            return tuple(new)

        sums = lax.fori_loop(0, cols // STEP, body,
                             tuple(jnp.zeros((8, rank), F32) for _ in range(NLAG)))
        ar0[...] = jnp.concatenate([s.sum(axis=0, keepdims=True) for s in sums], axis=0)
        ar_core.start()

    def adjoint():
        lags = all_lags()

        def tail(k, carry):
            t0 = pl.multiple_of(cols + k * STEP, STEP)
            total = error_tile(t0, lags)
            live = jnp.full(total.shape, has_next.astype(F32))
            err[pl.ds(t0, STEP), :] = jnp.where(live > 0, total, 0.0)
            return carry

        def body(k, carry):
            t0 = pl.multiple_of(k * STEP, STEP)
            base = pl.multiple_of(my_s * width + t0, STEP)
            adj = err[pl.ds(base, STEP), :]
            for j in range(NLAG):
                adj = adj - w_ref[pl.ds(j, 1), :] * err[pl.ds(base + lags[j], STEP), :]
            own[pl.ds(t0, STEP), :] += adj
            return carry

        lax.fori_loop(0, LAGMAX // STEP, tail, 0)
        lax.fori_loop(0, width // STEP, body, 0)

    for i in range(nz):
        if i == nz - 1:
            prior_start()
            if i >= 1:
                after_core(i - 1)
        tiles(i)
        if i == 0:
            base = 1 + 1 + (nz - 1) + (ns - 1)
            pl.semaphore_wait(barrier, base + has_other.astype(jnp.int32))

            @pl.when(has_next)
            def _():
                to_next.start()

            @pl.when(has_prev)
            def _():
                to_prev.start()
        core_copy(i).start()
        if i == nz - 1:
            for o in range(1, ns):
                value = tt[lax.rem(my_s + o, ns)].T
                for k in range(width // TILE):
                    tsend[o - 1, k], tstep[o - 1, k] = code(value[k * TILE:(k + 1) * TILE])
                for copy in tcopies[o - 1]:
                    copy.start()
        elif i >= 1:
            after_core(i - 1)
        if i >= 3:
            after_y(i - 3)
    ar_core.wait()
    ar1[...] = ar0[...] + arc[...]
    ar_y.start()
    after_core(nz - 1)
    if nz >= 3:
        after_y(nz - 3)
    own[...] = tt[my_s].T * scale_series
    adjoint()
    if nz >= 2:
        after_y(nz - 2)
    ar_y.wait()
    arz[z] = ar1[...] + ary[...]
    for copy in az:
        copy.start()
    after_y(nz - 1)
    for copies in tcopies:
        for copy in copies:
            copy.wait()
    for k in range(width // TILE):
        data = own[pl.ds(k * TILE, TILE), :]
        for o in range(1, ns):
            data = data + decode(trecv[o - 1, k], trstep[o - 1, k]) * scale_series
        out_t[pl.ds(k * TILE, TILE), :] = data
    for copy in az:
        copy.wait()
    total = arz[0]
    for k in range(1, nz):
        total = total + arz[k]
    out_a[...] = total * (-scale_time)
    total = s2[...]
    for i in range(nz - 1):
        for copy in z_copy(i):
            copy.wait()
        total = total + decode(zrx[i], zrstep[i])
    out_s[...] = total * scale_time


def put_out(*refs):
    sem = refs[-1]
    copies = [pltpu.make_async_copy(refs[k], refs[3 + k], sem.at[k]) for k in range(3)]
    for copy in copies:
        copy.start()
    for copy in copies:
        copy.wait()


def per_device(panel, series_factors, time_factors, ar_weights, tile_mask, lags):
    rows, cols = panel.shape
    rank = series_factors.shape[1]
    n = lax.axis_size("tm")
    ns = lax.axis_size("series")
    nz = n // 4
    block = rows // n
    width = cols // ns
    row_tile = min(2 * TILE, rows // nz)
    any_space = pl.BlockSpec(memory_space=pl.ANY)
    vmem = pl.BlockSpec(memory_space=pltpu.VMEM)
    dma = pltpu.SemaphoreType.DMA
    body = functools.partial(
        kernel, n, ns, 1.0 / math.sqrt(cols * n), 1.0 / math.sqrt(rows * ns), row_tile)
    shapes = ((block, rank), (width, rank), (NLAG, rank))
    results = pl.pallas_call(
        body,
        out_shape=tuple(pltpu.VMEM(shape, F32) for shape in shapes),
        in_specs=[any_space] * 6,
        out_specs=(vmem, vmem, vmem),
        scratch_shapes=[
            pltpu.SMEM((NLAG,), jnp.int32),
            pltpu.SMEM(tile_mask.shape[::-1], jnp.int32),
            pltpu.VMEM((NLAG, rank), F32),
            pltpu.VMEM((rows, cols), BF16),
            pltpu.VMEM((rows, rank), BF16),
            pltpu.VMEM((cols, rank), BF16),
            pltpu.VMEM((rows, rank), F32),
            pltpu.VMEM((ns, rank, width), F32),
            pltpu.VMEM((max(ns - 1, 1), width // TILE, TILE, rank), jnp.int16),
            pltpu.VMEM((max(ns - 1, 1), width // TILE, 8, rank), F32),
            pltpu.VMEM((width, rank), F32),
            pltpu.VMEM((max(ns - 1, 1), width // TILE, TILE, rank), jnp.int16),
            pltpu.VMEM((max(ns - 1, 1), width // TILE, 8, rank), F32),
            pltpu.VMEM((cols + 2 * LAGMAX, rank), F32),
            pltpu.VMEM((cols + LAGMAX, rank), F32),
            pltpu.VMEM((LAGMAX, rank), BF16),
            pltpu.VMEM((LAGMAX, rank), BF16),
            pltpu.VMEM((nz, 2, block, rank), F32),
            pltpu.VMEM((nz, block, rank), F32),
            pltpu.VMEM((nz, block, rank), jnp.int16),
            pltpu.VMEM((nz, 8, rank), F32),
            pltpu.VMEM((nz, block, rank), jnp.int16),
            pltpu.VMEM((nz, 8, rank), F32),
            pltpu.VMEM((block, rank), F32),
            pltpu.VMEM((max(nz - 1, 1), block, rank), jnp.int16),
            pltpu.VMEM((max(nz - 1, 1), 8, rank), F32),
            pltpu.VMEM((max(nz - 1, 1), block, rank), jnp.int16),
            pltpu.VMEM((max(nz - 1, 1), 8, rank), F32),
            pltpu.VMEM((NLAG, rank), F32),
            pltpu.VMEM((NLAG, rank), F32),
            pltpu.VMEM((NLAG, rank), F32),
            pltpu.VMEM((NLAG, rank), F32),
            pltpu.VMEM((nz, NLAG, rank), F32),
            dma((nz,)),
            dma((5,)),
            dma((2, 2)),
            dma((max(ns - 1, 1), 2)),
            dma((nz, 2)),
            dma((nz, 2)),
            dma((max(nz - 1, 1), 2)),
            dma((max(ns - 1, 1), 2)),
            dma((nz, 2)),
            dma((max(nz - 1, 1), 2)),
            dma((2,)),
            dma((2,)),
            dma((max(nz - 1, 1), 2)),
        ],
        compiler_params=pltpu.CompilerParams(collective_id=0, has_side_effects=True),
        name="factor_grad",
    )(lags, tile_mask.T, panel, series_factors, time_factors, ar_weights)
    return pl.pallas_call(
        put_out,
        out_shape=tuple(jax.ShapeDtypeStruct(shape, F32) for shape in shapes),
        in_specs=[vmem] * 3,
        out_specs=(any_space,) * 3,
        scratch_shapes=[dma((3,))],
        name="put_out",
    )(*[pltpu.with_memory_space_constraint(r, pltpu.VMEM) for r in results])


def solution(mesh):
    in_specs = (P("series", "tm"), P("series", None), P("tm", None), P(), P("series", "tm"), P())
    out_specs = (P(("series", "tm"), None), P(("tm", "series"), None), P())
    return jax.shard_map(
        per_device, mesh=mesh, in_specs=in_specs, out_specs=out_specs, check_vma=False
    )
```
